32 devices in a mesh: row: 8 (over y, x, core), col: 4 (over z).
Axes of the slice: x: 2, y: 2, z: 4, core: 2. Of those that a mesh axis runs over, the one named last changes fastest.
Arguments:
- left_panels: float32 [8, 4, 16, 128, 128], P('row', 'col'), may hold values from -6 to 6
- right_panels: float32 [2, 4, 8, 12, 128, 128], P(None, 'col', 'row'), may hold values from -0.25 to 0.25
- product_lists: int32 [8, 4, 8, 96, 3], P('row', 'col'), may hold values from -1 to 23, as said below
Outputs:
- product_blocks: float32 [8, 4, 24, 128, 128], P('row', 'col')
The draws below stay inside these ranges and needn't reach their ends.
Inputs may be any that keep to these rules, and one draw needn't show every extreme that they name: `product_lists`: each entry is (left slot < 16, right slot < 12, output slot < 24). In each list the first entries, at least half of 96 and at most 96, are live with distinct (left, right) pairs, the rest are -1 in all three columns; some list holds 96 live entries.
All inputs are finite; a program needn't handle non-finite values.
Results may differ from the reference program's by a relative error of at most 0.0003.
Values sent between devices are 32-bit elements; how exact they have to be, the bound alone decides.
A program may use at most 128 MiB of HBM per device.

```python
import jax
import jax.numpy as jnp
from jax import lax

BLK = 128
LCAP = 16
RCAP = 12
PCAP = 96
OCAP = 24
STEPS = 8
QP = 2
N_ROW = 8
N_COL = 4


def draw_product_lists(key, part):
    cells = N_ROW * N_COL * STEPS
    keys = jax.random.split(key, 6)
    pair_keys = jax.random.split(keys[0], cells)
    pairs = jax.vmap(lambda one_key: jax.random.permutation(one_key, LCAP * RCAP)[:PCAP])(pair_keys)
    out_slots = jax.random.randint(keys[1], (cells, PCAP), 0, OCAP)
    half_count = PCAP // 2
    first = jax.random.randint(keys[2], (cells,), 0, PCAP - half_count + 1)
    second = jax.random.randint(keys[3], (cells,), 0, PCAP - half_count + 1)
    counts = half_count + jnp.minimum(first, second)
    chosen = jax.random.randint(keys[5], (), 0, cells)
    counts = jnp.where(jnp.arange(cells) == chosen, PCAP, counts)
    live_mask = jnp.arange(PCAP)[None, :] < counts[:, None]
    left_col = jnp.where(live_mask, pairs // RCAP, -1)
    right_col = jnp.where(live_mask, pairs % RCAP, -1)
    out_col = jnp.where(live_mask, out_slots, -1)
    stacked = jnp.stack([left_col, right_col, out_col], axis=-1).astype(jnp.int32)
    return stacked.reshape(N_ROW, N_COL, STEPS, PCAP, 3)


def steps_of(rng, shape, pieces, low, top_value):
    factor_of, own = 1.0, jax.random.fold_in(rng, 6)
    for dim, shards_of in pieces:
        steps = jnp.exp(jax.random.uniform(jax.random.fold_in(own, dim), (shards_of,), jnp.float32, low / len(pieces), top_value / len(pieces)))
        factor_of = factor_of * jnp.repeat(steps, shape[dim] // shards_of).reshape([-1 if axis == dim else 1 for axis in range(len(shape))])
    return factor_of


def noise(rng, extent, scale, bound, cuts=(), kind=jnp.bfloat16):
    values = scale * jax.random.normal(rng, extent, jnp.float32)
    if cuts:
        values = values * steps_of(rng, extent, cuts, -0.22, 0.18)
    return jnp.clip(values, -bound, bound).astype(kind)


def setup_inputs(seed: int = 0) -> dict:
    seeds = jax.random.split(jax.random.key(seed), 4)
    left_panels = noise(seeds[0], (N_ROW, N_COL, LCAP, BLK, BLK), 1.0, 6.0, ((0, 8), (1, 4)), jnp.float32)
    right_panels = noise(seeds[1], (QP, N_COL, N_ROW, RCAP, BLK, BLK), (4 * BLK) ** -0.5, 0.25, ((1, 4), (2, 8)), jnp.float32)
    product_lists = draw_product_lists(jax.random.fold_in(seeds[3], 71), 0)
    return {"left_panels": left_panels, "right_panels": right_panels, "product_lists": product_lists}


def contribute(left_stack, right_panel, entries, slot_count):
    live_mask = entries[:, 0] >= 0
    left_slot = jnp.maximum(entries[:, 0], 0)
    right_slot = jnp.maximum(entries[:, 1], 0)
    taken_left = jnp.take(left_stack, left_slot, axis=0)
    taken_right = jnp.take(right_panel, right_slot, axis=0)
    blocks = jnp.einsum("pik,pkj->pij", taken_left, taken_right, precision=lax.Precision.HIGHEST)
    slot_ids = jnp.arange(slot_count, dtype=jnp.int32)
    onehot = ((entries[:, 2][None, :] == slot_ids[:, None]) & live_mask[None, :]).astype(blocks.dtype)
    return jnp.einsum("op,pij->oij", onehot, blocks, precision=lax.Precision.HIGHEST)


def reference(left_panels, right_panels, product_lists):
    def device_block(device_index):
        row_pos = device_index // N_COL
        col_pos = device_index % N_COL
        running = jnp.zeros((OCAP, BLK, BLK), left_panels.dtype)
        for step_num in range(STEPS):
            kgroup = (row_pos + col_pos + step_num) % N_ROW
            left_stack = left_panels[kgroup, col_pos]
            right_panel = right_panels[kgroup // N_COL, kgroup % N_COL, row_pos]
            running = running + contribute(left_stack, right_panel, product_lists[row_pos, col_pos, step_num], OCAP)
        return running

    results = lax.map(device_block, jnp.arange(N_ROW * N_COL, dtype=jnp.int32))
    return results.reshape(N_ROW, N_COL, OCAP, BLK, BLK)
```

```python
import functools

import jax
import jax.numpy as jnp
from jax import lax
from jax.experimental import pallas as pl
from jax.experimental.pallas import tpu as pltpu
from jax.sharding import PartitionSpec as P

OCAP = 24
UNROLL = 8
AHEAD = 3
MESH = pl.DeviceIdType.MESH


def prepare(entries, slot_count):
    count = entries.shape[1]
    live = entries[..., 0] >= 0
    slots = jnp.where(live, entries[..., 2], slot_count)
    key = slots * count + jnp.arange(count, dtype=jnp.int32)
    rank = jnp.sum((key[:, None, :] < key[:, :, None]).astype(jnp.int32), axis=2)
    place = rank[:, None, :] == jnp.arange(count, dtype=jnp.int32)[None, :, None]

    def arrange(values):
        return jnp.sum(jnp.where(place, values[:, None, :], 0), axis=2)

    left_slot = arrange(jnp.maximum(entries[..., 0], 0))
    right_slot = arrange(jnp.maximum(entries[..., 1], 0))
    out_slot = arrange(slots)
    before = jnp.concatenate([jnp.full_like(out_slot[:, :1], -1), out_slot[:, :-1]], axis=1)
    keep = (out_slot == before).astype(jnp.int32)
    ids = jnp.arange(slot_count, dtype=jnp.int32)[None, :, None]
    upto = jnp.sum((slots[:, None, :] <= ids).astype(jnp.int32), axis=2)
    here = jnp.sum((slots[:, None, :] == ids).astype(jnp.int32), axis=2)
    last = jnp.maximum(upto - 1, 0)
    valid = (here > 0).astype(jnp.int32)
    return left_slot, right_slot, keep, last, valid


def kernel(row_count, col_count, a_ref, b_ref, keep_ref, last_ref, valid_ref, left_ref, right_ref, out_ref,
           left_all, right_all, lhs, rhs, sums, zsend, zrecv, lsend, psend, lrecv, local_sem):
    row = lax.axis_index("row")
    col = lax.axis_index("col")
    q_count = right_ref.shape[0]
    left_blocks, blk = left_ref.shape[2], left_ref.shape[3]
    right_blocks = right_ref.shape[3]
    step_count, pair_count = a_ref.shape
    slot_count = last_ref.shape[1]
    groups = row_count // 2
    group, parity = row // 2, row % 2
    partner = group * 2 + 1 - parity

    barrier = pltpu.get_barrier_semaphore()
    for i in range(1, groups):
        peer = lax.rem(group + i, groups) * 2 + parity
        pl.semaphore_signal(barrier, inc=1, device_id=(peer, col), device_id_type=MESH)
    pl.semaphore_signal(barrier, inc=1, device_id=(partner, col), device_id_type=MESH)

    @pl.when(col > 0)
    def _():
        pl.semaphore_signal(barrier, inc=1, device_id=(row, col - 1), device_id_type=MESH)

    @pl.when(col < col_count - 1)
    def _():
        pl.semaphore_signal(barrier, inc=1, device_id=(row, col + 1), device_id_type=MESH)

    own = [pltpu.make_async_copy(left_ref.at[0, 0], left_all.at[row], local_sem.at[0])]
    for q in range(q_count):
        own.append(pltpu.make_async_copy(right_ref.at[q, 0, 0], right_all.at[q, col], local_sem.at[1 + q]))
    for copy in own:
        copy.start()

    ends = (col == 0).astype(jnp.int32) + (col == col_count - 1).astype(jnp.int32)
    pl.semaphore_wait(barrier, groups + 2 - ends)

    def along(direction, q, source, from_ref):
        return pltpu.make_async_remote_copy(
            src_ref=from_ref,
            dst_ref=right_all.at[q, source],
            send_sem=zsend.at[direction, q, source],
            recv_sem=zrecv.at[q, source],
            device_id=(row, col + (1 if direction else -1)),
            device_id_type=MESH,
        )

    def own_panel(direction, q):
        return along(direction, q, col, right_ref.at[q, 0, 0])

    def relayed(direction, q, source):
        return along(direction, q, source, right_all.at[q, source])

    def across(i):
        return pltpu.make_async_remote_copy(
            src_ref=left_ref.at[0, 0],
            dst_ref=left_all.at[row],
            send_sem=lsend.at[i],
            recv_sem=lrecv.at[row],
            device_id=(lax.rem(group + i, groups) * 2 + parity, col),
            device_id_type=MESH,
        )

    def handed(i):
        source = lax.rem(group + i, groups) * 2 + parity
        return pltpu.make_async_remote_copy(
            src_ref=left_ref.at[0, 0] if i == 0 else left_all.at[source],
            dst_ref=left_all.at[source],
            send_sem=psend.at[i],
            recv_sem=lrecv.at[source],
            device_id=(partner, col),
            device_id_type=MESH,
        )

    def arrived_left(source):
        return pltpu.make_async_remote_copy(
            src_ref=left_all.at[source],
            dst_ref=left_all.at[source],
            send_sem=psend.at[0],
            recv_sem=lrecv.at[source],
            device_id=(partner, col),
            device_id_type=MESH,
        )

    for q in range(q_count):
        @pl.when(col > 0)
        def _():
            own_panel(0, q).start()

        @pl.when(col < col_count - 1)
        def _():
            own_panel(1, q).start()

    for i in range(1, groups):
        across(i).start()
    handed(0).start()

    out_ref[...] = jnp.zeros_like(out_ref)
    rhs[:, blk:, blk:] = jnp.zeros((right_blocks, blk, blk), rhs.dtype)
    for copy in own:
        copy.wait()

    sides = jnp.minimum(col, col_count - 1 - col)

    def source_of(position):
        rest = position - 1
        distance = jnp.where(rest < 2 * sides, rest // 2 + 1, rest - sides + 1)
        lower = jnp.where(rest < 2 * sides, rest % 2 == 0, col * 2 > col_count - 1)
        shifted = jnp.where(lower, col - distance, col + distance)
        return jnp.where(position == 0, col, shifted)

    def relay(item):
        source, q = source_of(item // q_count), lax.rem(item, q_count)

        @pl.when(source != col)
        def _():
            relayed(0, q, source).wait_recv()

        @pl.when((source < col) & (col < col_count - 1))
        def _():
            relayed(1, q, source).start()

        @pl.when((source > col) & (col > 0))
        def _():
            relayed(0, q, source).start()

    first = min(2 * q_count, row_count)
    lax.fori_loop(q_count, first, lambda item, c: (relay(item), c)[1], 0)
    for i in range(1, groups):
        source = lax.rem(group + i, groups) * 2 + parity
        arrived_left(source).wait_recv()
        handed(i).start()
    for i in range(groups):
        arrived_left(lax.rem(group + i, groups) * 2 + 1 - parity).wait_recv()

    def job(item, carry):
        ahead = item + AHEAD

        @pl.when((ahead >= first) & (ahead < row_count))
        def _():
            relay(ahead)

        source, q = source_of(item // q_count), lax.rem(item, q_count)
        kgroup = q * col_count + source
        step = lax.rem(kgroup - row - col + 2 * row_count, row_count)

        @pl.when(step < step_count)
        def _():
            def split_left(i, c):
                x = left_all[kgroup, i]
                high = x.astype(jnp.bfloat16)
                lhs[i, :, :blk] = high
                lhs[i, :, blk:] = (x - high.astype(jnp.float32)).astype(jnp.bfloat16)
                return c

            def split_right(i, c):
                x = right_all[q, source, i]
                high = x.astype(jnp.bfloat16)
                rhs[i, :blk, :blk] = high
                rhs[i, blk:, :blk] = high
                rhs[i, :blk, blk:] = (x - high.astype(jnp.float32)).astype(jnp.bfloat16)
                return c

            lax.fori_loop(0, left_blocks, split_left, 0)
            lax.fori_loop(0, right_blocks, split_right, 0)

            def some(batch, total):
                for u in range(UNROLL):
                    p = batch * UNROLL + u
                    both = jnp.dot(lhs[a_ref[step, p]], rhs[b_ref[step, p]], preferred_element_type=jnp.float32)
                    total = total * keep_ref[step, p].astype(jnp.float32) + (both[:, :blk] + both[:, blk:])
                    sums[p] = total
                return total

            lax.fori_loop(0, pair_count // UNROLL, some, jnp.zeros((blk, blk), jnp.float32))

            def put(o, c):
                out_ref[o] = out_ref[o] + sums[last_ref[step, o]] * valid_ref[step, o].astype(jnp.float32)
                return c

            lax.fori_loop(0, slot_count, put, 0)

        return carry

    lax.fori_loop(0, row_count, job, 0)

    for q in range(q_count):
        @pl.when(col > 0)
        def _():
            own_panel(0, q).wait_send()

        @pl.when(col < col_count - 1)
        def _():
            own_panel(1, q).wait_send()

    def sent(item, carry):
        source, q = source_of(item // q_count), lax.rem(item, q_count)

        @pl.when((source < col) & (col < col_count - 1))
        def _():
            relayed(1, q, source).wait_send()

        @pl.when((source > col) & (col > 0))
        def _():
            relayed(0, q, source).wait_send()

        return carry

    lax.fori_loop(q_count, row_count, sent, 0)
    for i in range(1, groups):
        across(i).wait_send()
    for i in range(groups):
        handed(i).wait_send()


def shards(row_count, col_count, left_panels, right_panels, product_lists):
    left_blocks, blk = left_panels.shape[2], left_panels.shape[3]
    q_count, right_blocks = right_panels.shape[0], right_panels.shape[3]
    pair_count = product_lists.shape[3]
    lists = prepare(product_lists[0, 0], OCAP)
    groups = row_count // 2
    out = pl.pallas_call(
        functools.partial(kernel, row_count, col_count),
        out_shape=jax.ShapeDtypeStruct((OCAP, blk, blk), jnp.float32),
        in_specs=[pl.BlockSpec(memory_space=pltpu.SMEM)] * 5 + [pl.BlockSpec(memory_space=pl.ANY)] * 2,
        out_specs=pl.BlockSpec(memory_space=pltpu.VMEM),
        scratch_shapes=[
            pltpu.VMEM((row_count, left_blocks, blk, blk), jnp.float32),
            pltpu.VMEM((q_count, col_count, right_blocks, blk, blk), jnp.float32),
            pltpu.VMEM((left_blocks, blk, 2 * blk), jnp.bfloat16),
            pltpu.VMEM((right_blocks, 2 * blk, 2 * blk), jnp.bfloat16),
            pltpu.VMEM((pair_count, blk, blk), jnp.float32),
            pltpu.SemaphoreType.DMA((2, q_count, col_count)),
            pltpu.SemaphoreType.DMA((q_count, col_count)),
            pltpu.SemaphoreType.DMA((groups,)),
            pltpu.SemaphoreType.DMA((groups,)),
            pltpu.SemaphoreType.DMA((row_count,)),
            pltpu.SemaphoreType.DMA((1 + q_count,)),
        ],
        compiler_params=pltpu.CompilerParams(
            collective_id=0, has_side_effects=True, vmem_limit_bytes=60 * 1024 * 1024
        ),
    )(*lists, left_panels, right_panels)
    return out[None, None]


def solution(mesh):
    return jax.shard_map(
        functools.partial(shards, mesh.shape["row"], mesh.shape["col"]),
        mesh=mesh,
        in_specs=(
            P("row", "col", None, None, None),
            P(None, "col", "row", None, None, None),
            P("row", "col", None, None, None),
        ),
        out_specs=P("row", "col", None, None, None),
        check_vma=False,
    )
```

```python
import functools

import jax
import jax.numpy as jnp
from jax import lax
from jax.experimental import pallas as pl
from jax.experimental.pallas import tpu as pltpu
from jax.sharding import PartitionSpec as P

OCAP = 24
UNROLL = 8
AHEAD = 3
MESH = pl.DeviceIdType.MESH


def prepare(entries, slot_count):
    count = entries.shape[1]
    live = entries[..., 0] >= 0
    slots = jnp.where(live, entries[..., 2], slot_count)
    key = slots * count + jnp.arange(count, dtype=jnp.int32)
    rank = jnp.sum((key[:, None, :] < key[:, :, None]).astype(jnp.int32), axis=2)
    packed = jnp.where(live, entries[..., 0] + entries[..., 1] * 256, 0) + slots * 65536
    place = rank[:, None, :] == jnp.arange(count, dtype=jnp.int32)[None, :, None]
    codes = jnp.sum(jnp.where(place, packed[:, None, :], 0), axis=2)
    ids = jnp.arange(slot_count, dtype=jnp.int32)[None, :, None]
    upto = (slots[:, None, :] <= ids).astype(jnp.int32) + (slots[:, None, :] == ids).astype(jnp.int32) * 65536
    return codes, jnp.sum(upto, axis=2)


def kernel(row_count, col_count, code_ref, upto_ref, left_ref, right_ref, out_ref,
           left_all, right_all, lhs, rhs, sums, zsend, zrecv, lsend, psend, hsend, lrecv, hrecv, local_sem):
    row = lax.axis_index("row")
    col = lax.axis_index("col")
    q_count = right_ref.shape[0]
    left_blocks, blk = left_ref.shape[2], left_ref.shape[3]
    right_blocks = right_ref.shape[3]
    step_count, pair_count = code_ref.shape
    slot_count = upto_ref.shape[1]
    groups = row_count // 2
    group, parity = row // 2, row % 2
    partner = group * 2 + 1 - parity
    square = groups == 4
    direct = (1, 2) if square else tuple(range(1, groups))

    def group_at(i):
        return (group // 2 * 2 + 1 - group % 2 if i == 1 else lax.rem(group + 2, groups)) if square and i in (1, 2) else (
            groups - 1 - group if square and i == 3 else lax.rem(group + i, groups))

    def row_at(i, same):
        return group_at(i) * 2 + (parity if same else 1 - parity)

    barrier = pltpu.get_barrier_semaphore()
    for i in direct:
        pl.semaphore_signal(barrier, inc=1, device_id=(row_at(i, True), col), device_id_type=MESH)
    pl.semaphore_signal(barrier, inc=1, device_id=(partner, col), device_id_type=MESH)

    @pl.when(col > 0)
    def _():
        pl.semaphore_signal(barrier, inc=1, device_id=(row, col - 1), device_id_type=MESH)

    @pl.when(col < col_count - 1)
    def _():
        pl.semaphore_signal(barrier, inc=1, device_id=(row, col + 1), device_id_type=MESH)

    own = [pltpu.make_async_copy(left_ref.at[0, 0], left_all.at[row], local_sem.at[0])]
    for q in range(q_count):
        own.append(pltpu.make_async_copy(right_ref.at[q, 0, 0], right_all.at[q, col], local_sem.at[1 + q]))
    for copy in own:
        copy.start()

    ends = (col == 0).astype(jnp.int32) + (col == col_count - 1).astype(jnp.int32)
    pl.semaphore_wait(barrier, len(direct) + 3 - ends)

    def along(direction, q, source, from_ref):
        return pltpu.make_async_remote_copy(
            src_ref=from_ref,
            dst_ref=right_all.at[q, source],
            send_sem=zsend.at[direction, q, source],
            recv_sem=zrecv.at[q, source],
            device_id=(row, col + (1 if direction else -1)),
            device_id_type=MESH,
        )

    def own_panel(direction, q):
        return along(direction, q, col, right_ref.at[q, 0, 0])

    def relayed(direction, q, source):
        return along(direction, q, source, right_all.at[q, source])

    def across(i):
        return pltpu.make_async_remote_copy(
            src_ref=left_ref.at[0, 0],
            dst_ref=left_all.at[row],
            send_sem=lsend.at[i],
            recv_sem=lrecv.at[row],
            device_id=(row_at(i, True), col),
            device_id_type=MESH,
        )

    def handed(i):
        source = row_at(i, True)
        return pltpu.make_async_remote_copy(
            src_ref=left_ref.at[0, 0] if i == 0 else left_all.at[source],
            dst_ref=left_all.at[source],
            send_sem=psend.at[i],
            recv_sem=lrecv.at[source],
            device_id=(partner, col),
            device_id_type=MESH,
        )

    def arrived_left(source):
        return pltpu.make_async_remote_copy(
            src_ref=left_all.at[source],
            dst_ref=left_all.at[source],
            send_sem=psend.at[0],
            recv_sem=lrecv.at[source],
            device_id=(partner, col),
            device_id_type=MESH,
        )

    half = left_blocks // 2
    pieces = (pl.ds(0, half), pl.ds(half, left_blocks - half))

    def half_of(i, piece, target):
        source = row_at(i, True)
        return pltpu.make_async_remote_copy(
            src_ref=left_all.at[source, pieces[piece]],
            dst_ref=left_all.at[source, pieces[piece]],
            send_sem=hsend.at[piece],
            recv_sem=hrecv.at[piece],
            device_id=(row_at(target, True), col),
            device_id_type=MESH,
        )

    for q in range(q_count):
        @pl.when(col > 0)
        def _():
            own_panel(0, q).start()

        @pl.when(col < col_count - 1)
        def _():
            own_panel(1, q).start()

    for i in direct:
        across(i).start()
    handed(0).start()

    out_ref[...] = jnp.zeros_like(out_ref)
    rhs[:, blk:, blk:] = jnp.zeros((right_blocks, blk, blk), rhs.dtype)
    for copy in own:
        copy.wait()

    sides = jnp.minimum(col, col_count - 1 - col)

    def item_of(item):
        rest = item - q_count
        later = rest - 2 * q_count * sides
        both = later < 0
        distance = jnp.where(both, rest // (2 * q_count) + 1, sides + 1 + later // q_count)
        q = jnp.where(both, rest % (2 * q_count) // 2, later % q_count)
        lower = jnp.where(both, rest % 2 == 0, col * 2 > col_count - 1)
        source = jnp.where(lower, col - distance, col + distance)
        own_item = rest < 0
        return jnp.where(own_item, col, source), jnp.where(own_item, item, q)

    def relay(item):
        source, q = item_of(item)

        @pl.when(source != col)
        def _():
            relayed(0, q, source).wait_recv()

        @pl.when((source < col) & (col < col_count - 1))
        def _():
            relayed(1, q, source).start()

        @pl.when((source > col) & (col > 0))
        def _():
            relayed(0, q, source).start()

    forwards = 1 - ends
    first = q_count * (2 + jnp.minimum(sides, 1))

    def relay_many(start, stop):
        lax.fori_loop(start, stop, lambda item, c: (relay(item), c)[1], 0)

    for i in direct:
        arrived_left(row_at(i, True)).wait_recv()
        if square:
            half_of(i, i - 1, 3 - i).start()
        handed(i).start()
    relay_many(q_count, first)
    if square:
        half_of(3, 0, 1).wait_recv()
        half_of(3, 1, 1).wait_recv()
        handed(3).start()
    for i in range(groups):
        arrived_left(row_at(i, False)).wait_recv()

    def job(item, carry):
        source, q = item_of(item)
        kgroup = q * col_count + source
        step = lax.rem(kgroup - row - col + 2 * row_count, row_count)

        @pl.when(step < step_count)
        def _():
            def split_left(i, c):
                x = left_all[kgroup, i]
                high = x.astype(jnp.bfloat16)
                lhs[i, :, :blk] = high
                lhs[i, :, blk:] = (x - high.astype(jnp.float32)).astype(jnp.bfloat16)
                return c

            lax.fori_loop(0, left_blocks, split_left, 0)

        ahead = item + AHEAD * forwards

        @pl.when((ahead >= first) & (ahead < row_count))
        def _():
            relay(ahead)

        @pl.when(step < step_count)
        def _():
            def split_right(i, c):
                x = right_all[q, source, i]
                high = x.astype(jnp.bfloat16)
                rhs[i, :blk, :blk] = high
                rhs[i, blk:, :blk] = high
                rhs[i, :blk, blk:] = (x - high.astype(jnp.float32)).astype(jnp.bfloat16)
                return c

            lax.fori_loop(0, right_blocks, split_right, 0)

            def some(batch, carry):
                total, before = carry
                for u in range(UNROLL):
                    p = batch * UNROLL + u
                    code = code_ref[step, p]
                    both = jnp.dot(
                        lhs[code & 255], rhs[(code >> 8) & 255], preferred_element_type=jnp.float32
                    )
                    slot = code >> 16
                    keep = (slot == before).astype(jnp.float32)
                    total = total * keep + (both[:, :blk] + both[:, blk:])
                    sums[p] = total
                    before = slot
                return total, before

            lax.fori_loop(0, pair_count // UNROLL, some, (jnp.zeros((blk, blk), jnp.float32), jnp.int32(-1)))

            def put(o, c):
                code = upto_ref[step, o]
                found = ((code >> 16) > 0).astype(jnp.float32)
                out_ref[o] = out_ref[o] + sums[jnp.maximum((code & 65535) - 1, 0)] * found
                return c

            lax.fori_loop(0, slot_count, put, 0)

        return carry

    lax.fori_loop(0, row_count, job, 0)

    for q in range(q_count):
        @pl.when(col > 0)
        def _():
            own_panel(0, q).wait_send()

        @pl.when(col < col_count - 1)
        def _():
            own_panel(1, q).wait_send()

    def sent(item, carry):
        source, q = item_of(item)

        @pl.when((source < col) & (col < col_count - 1))
        def _():
            relayed(1, q, source).wait_send()

        @pl.when((source > col) & (col > 0))
        def _():
            relayed(0, q, source).wait_send()

        return carry

    lax.fori_loop(q_count, row_count, sent, 0)
    for i in direct:
        across(i).wait_send()
    if square:
        half_of(1, 0, 2).wait_send()
        half_of(2, 1, 1).wait_send()
    for i in range(groups):
        handed(i).wait_send()


def shards(row_count, col_count, left_panels, right_panels, product_lists):
    left_blocks, blk = left_panels.shape[2], left_panels.shape[3]
    q_count, right_blocks = right_panels.shape[0], right_panels.shape[3]
    pair_count = product_lists.shape[3]
    lists = prepare(product_lists[0, 0], OCAP)
    groups = row_count // 2
    out = pl.pallas_call(
        functools.partial(kernel, row_count, col_count),
        out_shape=jax.ShapeDtypeStruct((OCAP, blk, blk), jnp.float32),
        in_specs=[pl.BlockSpec(memory_space=pltpu.SMEM)] * 2 + [pl.BlockSpec(memory_space=pl.ANY)] * 2,
        out_specs=pl.BlockSpec(memory_space=pltpu.VMEM),
        scratch_shapes=[
            pltpu.VMEM((row_count, left_blocks, blk, blk), jnp.float32),
            pltpu.VMEM((q_count, col_count, right_blocks, blk, blk), jnp.float32),
            pltpu.VMEM((left_blocks, blk, 2 * blk), jnp.bfloat16),
            pltpu.VMEM((right_blocks, 2 * blk, 2 * blk), jnp.bfloat16),
            pltpu.VMEM((pair_count, blk, blk), jnp.float32),
            pltpu.SemaphoreType.DMA((2, q_count, col_count)),
            pltpu.SemaphoreType.DMA((q_count, col_count)),
            pltpu.SemaphoreType.DMA((groups,)),
            pltpu.SemaphoreType.DMA((groups,)),
            pltpu.SemaphoreType.DMA((2,)),
            pltpu.SemaphoreType.DMA((row_count,)),
            pltpu.SemaphoreType.DMA((2,)),
            pltpu.SemaphoreType.DMA((1 + q_count,)),
        ],
        compiler_params=pltpu.CompilerParams(
            collective_id=0, has_side_effects=True, vmem_limit_bytes=60 * 1024 * 1024
        ),
    )(*lists, left_panels, right_panels)
    return out[None, None]


def solution(mesh):
    return jax.shard_map(
        functools.partial(shards, mesh.shape["row"], mesh.shape["col"]),
        mesh=mesh,
        in_specs=(
            P("row", "col", None, None, None),
            P(None, "col", "row", None, None, None),
            P("row", "col", None, None, None),
        ),
        out_specs=P("row", "col", None, None, None),
        check_vma=False,
    )
```

```python
import functools

import jax
import jax.numpy as jnp
from jax import lax
from jax.experimental import pallas as pl
from jax.experimental.pallas import tpu as pltpu
from jax.sharding import PartitionSpec as P

OCAP = 24
UNROLL = 8
AHEAD = 3
MESH = pl.DeviceIdType.MESH


def arrange(lists_ref, table, step, slot_count):
    step_count, count = lists_ref.shape[1], lists_ref.shape[2]
    width = table.shape[1]
    left, right, out = (lists_ref[part, pl.ds(step, 1), :] for part in range(3))
    live = left >= 0
    slots = jnp.where(live, out, slot_count)
    lane = lax.broadcasted_iota(jnp.int32, (count, count), 1)
    same = lax.broadcasted_iota(jnp.int32, (count, count), 0) == lane

    def column(row):
        return jnp.sum(jnp.where(same, jnp.broadcast_to(row, (count, count)), 0), axis=1, keepdims=True)

    key = jnp.broadcast_to(slots, (count, count)) * count + lane
    key_column = jnp.sum(jnp.where(same, key, 0), axis=1, keepdims=True)
    rank = jnp.sum((key < key_column).astype(jnp.int32), axis=1, keepdims=True)
    packed = column(jnp.where(live, left + right * 256, 0) + slots * 65536)
    wide = lax.broadcasted_iota(jnp.int32, (count, width), 1)
    table[pl.ds(step, 1), :] = jnp.sum(jnp.where(rank == wide, packed, 0), axis=0, keepdims=True)
    slot_column = column(slots)
    upto = (slot_column <= wide).astype(jnp.int32) + (slot_column == wide).astype(jnp.int32) * 65536
    table[pl.ds(step_count + step, 1), :] = jnp.sum(upto, axis=0, keepdims=True)


def kernel(row_count, col_count, lists_ref, left_ref, right_ref, out_ref,
           left_all, right_all, lhs, rhs, sums, table, code_ref, zsend, zrecv, lsend, psend, hsend, lrecv, hrecv, local_sem):
    row = lax.axis_index("row")
    col = lax.axis_index("col")
    q_count = right_ref.shape[0]
    left_blocks, blk = left_ref.shape[2], left_ref.shape[3]
    right_blocks = right_ref.shape[3]
    step_count, pair_count = lists_ref.shape[1], lists_ref.shape[2]
    slot_count = out_ref.shape[0]
    groups = row_count // 2
    group, parity = row // 2, row % 2
    partner = group * 2 + 1 - parity
    square = groups == 4
    direct = (1, 2) if square else tuple(range(1, groups))

    def group_at(i):
        return (group // 2 * 2 + 1 - group % 2 if i == 1 else lax.rem(group + 2, groups)) if square and i in (1, 2) else (
            groups - 1 - group if square and i == 3 else lax.rem(group + i, groups))

    def row_at(i, same):
        return group_at(i) * 2 + (parity if same else 1 - parity)

    barrier = pltpu.get_barrier_semaphore()
    for i in direct:
        pl.semaphore_signal(barrier, inc=1, device_id=(row_at(i, True), col), device_id_type=MESH)
    pl.semaphore_signal(barrier, inc=1, device_id=(partner, col), device_id_type=MESH)

    @pl.when(col > 0)
    def _():
        pl.semaphore_signal(barrier, inc=1, device_id=(row, col - 1), device_id_type=MESH)

    @pl.when(col < col_count - 1)
    def _():
        pl.semaphore_signal(barrier, inc=1, device_id=(row, col + 1), device_id_type=MESH)

    own = [pltpu.make_async_copy(left_ref.at[0, 0], left_all.at[row], local_sem.at[0])]
    for q in range(q_count):
        own.append(pltpu.make_async_copy(right_ref.at[q, 0, 0], right_all.at[q, col], local_sem.at[1 + q]))
    for copy in own:
        copy.start()

    ends = (col == 0).astype(jnp.int32) + (col == col_count - 1).astype(jnp.int32)
    pl.semaphore_wait(barrier, len(direct) + 3 - ends)

    def along(direction, q, source, from_ref):
        return pltpu.make_async_remote_copy(
            src_ref=from_ref,
            dst_ref=right_all.at[q, source],
            send_sem=zsend.at[direction, q, source],
            recv_sem=zrecv.at[q, source],
            device_id=(row, col + (1 if direction else -1)),
            device_id_type=MESH,
        )

    def own_panel(direction, q):
        return along(direction, q, col, right_ref.at[q, 0, 0])

    def relayed(direction, q, source):
        return along(direction, q, source, right_all.at[q, source])

    def across(i):
        return pltpu.make_async_remote_copy(
            src_ref=left_ref.at[0, 0],
            dst_ref=left_all.at[row],
            send_sem=lsend.at[i],
            recv_sem=lrecv.at[row],
            device_id=(row_at(i, True), col),
            device_id_type=MESH,
        )

    def handed(i):
        source = row_at(i, True)
        return pltpu.make_async_remote_copy(
            src_ref=left_ref.at[0, 0] if i == 0 else left_all.at[source],
            dst_ref=left_all.at[source],
            send_sem=psend.at[i],
            recv_sem=lrecv.at[source],
            device_id=(partner, col),
            device_id_type=MESH,
        )

    def arrived_left(source):
        return pltpu.make_async_remote_copy(
            src_ref=left_all.at[source],
            dst_ref=left_all.at[source],
            send_sem=psend.at[0],
            recv_sem=lrecv.at[source],
            device_id=(partner, col),
            device_id_type=MESH,
        )

    half = left_blocks // 2
    pieces = (pl.ds(0, half), pl.ds(half, left_blocks - half))

    def half_of(i, piece, target):
        source = row_at(i, True)
        return pltpu.make_async_remote_copy(
            src_ref=left_all.at[source, pieces[piece]],
            dst_ref=left_all.at[source, pieces[piece]],
            send_sem=hsend.at[piece],
            recv_sem=hrecv.at[piece],
            device_id=(row_at(target, True), col),
            device_id_type=MESH,
        )

    for q in range(q_count):
        @pl.when(col > 0)
        def _():
            own_panel(0, q).start()

        @pl.when(col < col_count - 1)
        def _():
            own_panel(1, q).start()

    for i in direct:
        across(i).start()
    handed(0).start()

    lax.fori_loop(0, step_count, lambda step, c: (arrange(lists_ref, table, step, slot_count), c)[1], 0)
    out_ref[...] = jnp.zeros_like(out_ref)
    rhs[:, blk:, blk:] = jnp.zeros((right_blocks, blk, blk), rhs.dtype)
    for copy in own:
        copy.wait()

    sides = jnp.minimum(col, col_count - 1 - col)

    def item_of(item):
        rest = item - q_count
        later = rest - 2 * q_count * sides
        both = later < 0
        distance = jnp.where(both, rest // (2 * q_count) + 1, sides + 1 + later // q_count)
        q = jnp.where(both, rest % (2 * q_count) // 2, later % q_count)
        lower = jnp.where(both, rest % 2 == 0, col * 2 > col_count - 1)
        source = jnp.where(lower, col - distance, col + distance)
        own_item = rest < 0
        return jnp.where(own_item, col, source), jnp.where(own_item, item, q)

    def relay(item):
        source, q = item_of(item)

        @pl.when(source != col)
        def _():
            relayed(0, q, source).wait_recv()

        @pl.when((source < col) & (col < col_count - 1))
        def _():
            relayed(1, q, source).start()

        @pl.when((source > col) & (col > 0))
        def _():
            relayed(0, q, source).start()

    forwards = 1 - ends
    first = q_count * (2 + jnp.minimum(sides, 1))

    def relay_many(start, stop):
        lax.fori_loop(start, stop, lambda item, c: (relay(item), c)[1], 0)

    for i in direct:
        arrived_left(row_at(i, True)).wait_recv()
        if square:
            half_of(i, i - 1, 3 - i).start()
        handed(i).start()
    relay_many(q_count, first)
    listed = pltpu.make_async_copy(table, code_ref, local_sem.at[1 + q_count])
    listed.start()
    if square:
        half_of(3, 0, 1).wait_recv()
        half_of(3, 1, 1).wait_recv()
        handed(3).start()
    for i in range(groups):
        arrived_left(row_at(i, False)).wait_recv()
    listed.wait()

    def job(item, carry):
        source, q = item_of(item)
        kgroup = q * col_count + source
        step = lax.rem(kgroup - row - col + 2 * row_count, row_count)

        @pl.when(step < step_count)
        def _():
            def split_left(i, c):
                x = left_all[kgroup, i]
                high = x.astype(jnp.bfloat16)
                lhs[i, :, :blk] = high
                lhs[i, :, blk:] = (x - high.astype(jnp.float32)).astype(jnp.bfloat16)
                return c

            lax.fori_loop(0, left_blocks, split_left, 0)

        ahead = item + AHEAD * forwards

        @pl.when((ahead >= first) & (ahead < row_count))
        def _():
            relay(ahead)

        @pl.when(step < step_count)
        def _():
            def split_right(i, c):
                x = right_all[q, source, i]
                high = x.astype(jnp.bfloat16)
                rhs[i, :blk, :blk] = high
                rhs[i, blk:, :blk] = high
                rhs[i, :blk, blk:] = (x - high.astype(jnp.float32)).astype(jnp.bfloat16)
                return c

            lax.fori_loop(0, right_blocks, split_right, 0)

            def some(batch, carry):
                total, before = carry
                for u in range(UNROLL):
                    p = batch * UNROLL + u
                    code = code_ref[step, p]
                    both = jnp.dot(
                        lhs[code & 255], rhs[(code >> 8) & 255], preferred_element_type=jnp.float32
                    )
                    slot = code >> 16
                    keep = (slot == before).astype(jnp.float32)
                    total = total * keep + (both[:, :blk] + both[:, blk:])
                    sums[p] = total
                    before = slot
                return total, before

            lax.fori_loop(0, pair_count // UNROLL, some, (jnp.zeros((blk, blk), jnp.float32), jnp.int32(-1)))

            def put(o, c):
                code = code_ref[step_count + step, o]
                found = ((code >> 16) > 0).astype(jnp.float32)
                out_ref[o] = out_ref[o] + sums[jnp.maximum((code & 65535) - 1, 0)] * found
                return c

            lax.fori_loop(0, slot_count, put, 0)

        return carry

    lax.fori_loop(0, row_count, job, 0)

    for q in range(q_count):
        @pl.when(col > 0)
        def _():
            own_panel(0, q).wait_send()

        @pl.when(col < col_count - 1)
        def _():
            own_panel(1, q).wait_send()

    def sent(item, carry):
        source, q = item_of(item)

        @pl.when((source < col) & (col < col_count - 1))
        def _():
            relayed(1, q, source).wait_send()

        @pl.when((source > col) & (col > 0))
        def _():
            relayed(0, q, source).wait_send()

        return carry

    lax.fori_loop(q_count, row_count, sent, 0)
    for i in direct:
        across(i).wait_send()
    if square:
        half_of(1, 0, 2).wait_send()
        half_of(2, 1, 1).wait_send()
    for i in range(groups):
        handed(i).wait_send()


def shards(row_count, col_count, left_panels, right_panels, product_lists):
    left_blocks, blk = left_panels.shape[2], left_panels.shape[3]
    q_count, right_blocks = right_panels.shape[0], right_panels.shape[3]
    pair_count = product_lists.shape[3]
    lists = jnp.transpose(product_lists[0, 0], (2, 0, 1))
    step_count = lists.shape[1]
    width = pl.cdiv(max(pair_count, OCAP), 128) * 128
    groups = row_count // 2
    out = pl.pallas_call(
        functools.partial(kernel, row_count, col_count),
        out_shape=jax.ShapeDtypeStruct((OCAP, blk, blk), jnp.float32),
        in_specs=[pl.BlockSpec(memory_space=pltpu.VMEM)] + [pl.BlockSpec(memory_space=pltpu.HBM)] * 2,
        out_specs=pl.BlockSpec(memory_space=pltpu.VMEM),
        scratch_shapes=[
            pltpu.VMEM((row_count, left_blocks, blk, blk), jnp.float32),
            pltpu.VMEM((q_count, col_count, right_blocks, blk, blk), jnp.float32),
            pltpu.VMEM((left_blocks, blk, 2 * blk), jnp.bfloat16),
            pltpu.VMEM((right_blocks, 2 * blk, 2 * blk), jnp.bfloat16),
            pltpu.VMEM((pair_count, blk, blk), jnp.float32),
            pltpu.VMEM((2 * step_count, width), jnp.int32),
            pltpu.SMEM((2 * step_count, width), jnp.int32),
            pltpu.SemaphoreType.DMA((2, q_count, col_count)),
            pltpu.SemaphoreType.DMA((q_count, col_count)),
            pltpu.SemaphoreType.DMA((groups,)),
            pltpu.SemaphoreType.DMA((groups,)),
            pltpu.SemaphoreType.DMA((2,)),
            pltpu.SemaphoreType.DMA((row_count,)),
            pltpu.SemaphoreType.DMA((2,)),
            pltpu.SemaphoreType.DMA((2 + q_count,)),
        ],
        compiler_params=pltpu.CompilerParams(
            collective_id=0, has_side_effects=True, vmem_limit_bytes=50 * 1024 * 1024
        ),
    )(lists, left_panels, right_panels)
    return out[None, None]


def solution(mesh):
    return jax.shard_map(
        functools.partial(shards, mesh.shape["row"], mesh.shape["col"]),
        mesh=mesh,
        in_specs=(
            P("row", "col", None, None, None),
            P(None, "col", "row", None, None, None),
            P("row", "col", None, None, None),
        ),
        out_specs=P("row", "col", None, None, None),
        check_vma=False,
    )
```

```python
import functools

import jax
import jax.numpy as jnp
from jax import lax
from jax.experimental import pallas as pl
from jax.experimental.pallas import tpu as pltpu
from jax.sharding import PartitionSpec as P

OCAP = 24
UNROLL = 16
AHEAD = 3
MESH = pl.DeviceIdType.MESH


def arrange(lists_ref, table, step, slot_count):
    step_count, count = lists_ref.shape[1], lists_ref.shape[2]
    width = table.shape[1]
    left, right, out = (lists_ref[part, pl.ds(step, 1), :] for part in range(3))
    live = left >= 0
    slots = jnp.where(live, out, slot_count)
    lane = lax.broadcasted_iota(jnp.int32, (count, count), 1)
    same = lax.broadcasted_iota(jnp.int32, (count, count), 0) == lane

    def column(row):
        return jnp.sum(jnp.where(same, jnp.broadcast_to(row, (count, count)), 0), axis=1, keepdims=True)

    key = jnp.broadcast_to(slots, (count, count)) * count + lane
    key_column = jnp.sum(jnp.where(same, key, 0), axis=1, keepdims=True)
    rank = jnp.sum((key < key_column).astype(jnp.int32), axis=1, keepdims=True)
    packed = column(jnp.where(live, left + right * 256, 0) + slots * 65536)
    wide = lax.broadcasted_iota(jnp.int32, (count, width), 1)
    table[pl.ds(step, 1), :] = jnp.sum(jnp.where(rank == wide, packed, 0), axis=0, keepdims=True)
    slot_column = column(slots)
    upto = (slot_column <= wide).astype(jnp.int32) + (slot_column == wide).astype(jnp.int32) * 65536
    table[pl.ds(step_count + step, 1), :] = jnp.sum(upto, axis=0, keepdims=True)


def kernel(row_count, col_count, lists_ref, left_ref, right_ref, out_ref,
           left_all, right_all, lhs, rhs, sums, table, code_ref, zsend, zrecv, lsend, psend, hsend, lrecv, hrecv, local_sem):
    row = lax.axis_index("row")
    col = lax.axis_index("col")
    q_count = right_ref.shape[0]
    left_blocks, blk = left_ref.shape[2], left_ref.shape[3]
    right_blocks = right_ref.shape[3]
    step_count, pair_count = lists_ref.shape[1], lists_ref.shape[2]
    slot_count = out_ref.shape[0]
    groups = row_count // 2
    group, parity = row // 2, row % 2
    partner = group * 2 + 1 - parity
    square = groups == 4
    direct = (1, 2) if square else tuple(range(1, groups))

    def group_at(i):
        return (group // 2 * 2 + 1 - group % 2 if i == 1 else lax.rem(group + 2, groups)) if square and i in (1, 2) else (
            groups - 1 - group if square and i == 3 else lax.rem(group + i, groups))

    def row_at(i, same):
        return group_at(i) * 2 + (parity if same else 1 - parity)

    barrier = pltpu.get_barrier_semaphore()
    for i in direct:
        pl.semaphore_signal(barrier, inc=1, device_id=(row_at(i, True), col), device_id_type=MESH)
    pl.semaphore_signal(barrier, inc=1, device_id=(partner, col), device_id_type=MESH)

    @pl.when(col > 0)
    def _():
        pl.semaphore_signal(barrier, inc=1, device_id=(row, col - 1), device_id_type=MESH)

    @pl.when(col < col_count - 1)
    def _():
        pl.semaphore_signal(barrier, inc=1, device_id=(row, col + 1), device_id_type=MESH)

    own = [pltpu.make_async_copy(left_ref.at[0, 0], left_all.at[row], local_sem.at[0])]
    for q in range(q_count):
        own.append(pltpu.make_async_copy(right_ref.at[q, 0, 0], right_all.at[q, col], local_sem.at[1 + q]))
    for copy in own:
        copy.start()

    ends = (col == 0).astype(jnp.int32) + (col == col_count - 1).astype(jnp.int32)
    pl.semaphore_wait(barrier, len(direct) + 3 - ends)

    def along(direction, q, source, from_ref):
        return pltpu.make_async_remote_copy(
            src_ref=from_ref,
            dst_ref=right_all.at[q, source],
            send_sem=zsend.at[direction, q, source],
            recv_sem=zrecv.at[q, source],
            device_id=(row, col + (1 if direction else -1)),
            device_id_type=MESH,
        )

    def own_panel(direction, q):
        return along(direction, q, col, right_ref.at[q, 0, 0])

    def relayed(direction, q, source):
        return along(direction, q, source, right_all.at[q, source])

    def across(i):
        return pltpu.make_async_remote_copy(
            src_ref=left_ref.at[0, 0],
            dst_ref=left_all.at[row],
            send_sem=lsend.at[i],
            recv_sem=lrecv.at[row],
            device_id=(row_at(i, True), col),
            device_id_type=MESH,
        )

    def handed(i):
        source = row_at(i, True)
        return pltpu.make_async_remote_copy(
            src_ref=left_ref.at[0, 0] if i == 0 else left_all.at[source],
            dst_ref=left_all.at[source],
            send_sem=psend.at[i],
            recv_sem=lrecv.at[source],
            device_id=(partner, col),
            device_id_type=MESH,
        )

    def arrived_left(source):
        return pltpu.make_async_remote_copy(
            src_ref=left_all.at[source],
            dst_ref=left_all.at[source],
            send_sem=psend.at[0],
            recv_sem=lrecv.at[source],
            device_id=(partner, col),
            device_id_type=MESH,
        )

    half = left_blocks // 2
    pieces = (pl.ds(0, half), pl.ds(half, left_blocks - half))

    def half_of(i, piece, target):
        source = row_at(i, True)
        return pltpu.make_async_remote_copy(
            src_ref=left_all.at[source, pieces[piece]],
            dst_ref=left_all.at[source, pieces[piece]],
            send_sem=hsend.at[piece],
            recv_sem=hrecv.at[piece],
            device_id=(row_at(target, True), col),
            device_id_type=MESH,
        )

    for q in range(q_count):
        @pl.when(col > 0)
        def _():
            own_panel(0, q).start()

        @pl.when(col < col_count - 1)
        def _():
            own_panel(1, q).start()

    for i in direct:
        across(i).start()
    handed(0).start()

    lax.fori_loop(0, step_count, lambda step, c: (arrange(lists_ref, table, step, slot_count), c)[1], 0)
    out_ref[...] = jnp.zeros_like(out_ref)
    rhs[:, blk:, blk:] = jnp.zeros((right_blocks, blk, blk), rhs.dtype)
    for copy in own:
        copy.wait()

    sides = jnp.minimum(col, col_count - 1 - col)

    def item_of(item):
        rest = item - q_count
        later = rest - 2 * q_count * sides
        both = later < 0
        distance = jnp.where(both, rest // (2 * q_count) + 1, sides + 1 + later // q_count)
        q = jnp.where(both, rest % (2 * q_count) // 2, later % q_count)
        lower = jnp.where(both, rest % 2 == 0, col * 2 > col_count - 1)
        source = jnp.where(lower, col - distance, col + distance)
        own_item = rest < 0
        return jnp.where(own_item, col, source), jnp.where(own_item, item, q)

    def relay(item):
        source, q = item_of(item)

        @pl.when(source != col)
        def _():
            relayed(0, q, source).wait_recv()

        @pl.when((source < col) & (col < col_count - 1))
        def _():
            relayed(1, q, source).start()

        @pl.when((source > col) & (col > 0))
        def _():
            relayed(0, q, source).start()

    forwards = 1 - ends
    first = q_count * (2 + jnp.minimum(sides, 1))

    def relay_many(start, stop):
        lax.fori_loop(start, stop, lambda item, c: (relay(item), c)[1], 0)

    for i in direct:
        arrived_left(row_at(i, True)).wait_recv()
        if square:
            half_of(i, i - 1, 3 - i).start()
        handed(i).start()
    relay_many(q_count, first)
    listed = pltpu.make_async_copy(table, code_ref, local_sem.at[1 + q_count])
    listed.start()
    if square:
        half_of(3, 0, 1).wait_recv()
        half_of(3, 1, 1).wait_recv()
        handed(3).start()
    for i in range(groups):
        arrived_left(row_at(i, False)).wait_recv()
    listed.wait()

    def job(item, carry):
        source, q = item_of(item)
        kgroup = q * col_count + source
        step = lax.rem(kgroup - row - col + 2 * row_count, row_count)

        @pl.when(step < step_count)
        def _():
            def split_left(i, c):
                x = left_all[kgroup, i]
                high = x.astype(jnp.bfloat16)
                lhs[i, :, :blk] = high
                lhs[i, :, blk:] = (x - high.astype(jnp.float32)).astype(jnp.bfloat16)
                return c

            lax.fori_loop(0, left_blocks, split_left, 0)

        ahead = item + AHEAD * forwards

        @pl.when((ahead >= first) & (ahead < row_count))
        def _():
            relay(ahead)

        @pl.when(step < step_count)
        def _():
            def split_right(i, c):
                x = right_all[q, source, i]
                high = x.astype(jnp.bfloat16)
                rhs[i, :blk, :blk] = high
                rhs[i, blk:, :blk] = high
                rhs[i, :blk, blk:] = (x - high.astype(jnp.float32)).astype(jnp.bfloat16)
                return c

            lax.fori_loop(0, right_blocks, split_right, 0)

            def some(batch, carry):
                total, before = carry
                for u in range(UNROLL):
                    p = batch * UNROLL + u
                    code = code_ref[step, p]
                    both = jnp.dot(
                        lhs[code & 255], rhs[(code >> 8) & 255], preferred_element_type=jnp.float32
                    )
                    slot = code >> 16
                    keep = (slot == before).astype(jnp.float32)
                    total = total * keep + (both[:, :blk] + both[:, blk:])
                    sums[p] = total
                    before = slot
                return total, before

            lax.fori_loop(0, pair_count // UNROLL, some, (jnp.zeros((blk, blk), jnp.float32), jnp.int32(-1)))

            def put(o, c):
                code = code_ref[step_count + step, o]
                found = ((code >> 16) > 0).astype(jnp.float32)
                out_ref[o] = out_ref[o] + sums[jnp.maximum((code & 65535) - 1, 0)] * found
                return c

            lax.fori_loop(0, slot_count, put, 0)

        return carry

    lax.fori_loop(0, row_count, job, 0)

    for q in range(q_count):
        @pl.when(col > 0)
        def _():
            own_panel(0, q).wait_send()

        @pl.when(col < col_count - 1)
        def _():
            own_panel(1, q).wait_send()

    def sent(item, carry):
        source, q = item_of(item)

        @pl.when((source < col) & (col < col_count - 1))
        def _():
            relayed(1, q, source).wait_send()

        @pl.when((source > col) & (col > 0))
        def _():
            relayed(0, q, source).wait_send()

        return carry

    lax.fori_loop(q_count, row_count, sent, 0)
    for i in direct:
        across(i).wait_send()
    if square:
        half_of(1, 0, 2).wait_send()
        half_of(2, 1, 1).wait_send()
    for i in range(groups):
        handed(i).wait_send()


def shards(row_count, col_count, left_panels, right_panels, product_lists):
    left_blocks, blk = left_panels.shape[2], left_panels.shape[3]
    q_count, right_blocks = right_panels.shape[0], right_panels.shape[3]
    pair_count = product_lists.shape[3]
    lists = jnp.transpose(product_lists[0, 0], (2, 0, 1))
    step_count = lists.shape[1]
    width = pl.cdiv(max(pair_count, OCAP), 128) * 128
    groups = row_count // 2
    out = pl.pallas_call(
        functools.partial(kernel, row_count, col_count),
        out_shape=jax.ShapeDtypeStruct((OCAP, blk, blk), jnp.float32),
        in_specs=[pl.BlockSpec(memory_space=pltpu.VMEM)] + [pl.BlockSpec(memory_space=pltpu.HBM)] * 2,
        out_specs=pl.BlockSpec(memory_space=pltpu.VMEM),
        scratch_shapes=[
            pltpu.VMEM((row_count, left_blocks, blk, blk), jnp.float32),
            pltpu.VMEM((q_count, col_count, right_blocks, blk, blk), jnp.float32),
            pltpu.VMEM((left_blocks, blk, 2 * blk), jnp.bfloat16),
            pltpu.VMEM((right_blocks, 2 * blk, 2 * blk), jnp.bfloat16),
            pltpu.VMEM((pair_count, blk, blk), jnp.float32),
            pltpu.VMEM((2 * step_count, width), jnp.int32),
            pltpu.SMEM((2 * step_count, width), jnp.int32),
            pltpu.SemaphoreType.DMA((2, q_count, col_count)),
            pltpu.SemaphoreType.DMA((q_count, col_count)),
            pltpu.SemaphoreType.DMA((groups,)),
            pltpu.SemaphoreType.DMA((groups,)),
            pltpu.SemaphoreType.DMA((2,)),
            pltpu.SemaphoreType.DMA((row_count,)),
            pltpu.SemaphoreType.DMA((2,)),
            pltpu.SemaphoreType.DMA((2 + q_count,)),
        ],
        compiler_params=pltpu.CompilerParams(
            collective_id=0, has_side_effects=True, vmem_limit_bytes=50 * 1024 * 1024
        ),
    )(lists, left_panels, right_panels)
    return out[None, None]


def solution(mesh):
    return jax.shard_map(
        functools.partial(shards, mesh.shape["row"], mesh.shape["col"]),
        mesh=mesh,
        in_specs=(
            P("row", "col", None, None, None),
            P(None, "col", "row", None, None, None),
            P("row", "col", None, None, None),
        ),
        out_specs=P("row", "col", None, None, None),
        check_vma=False,
    )
```
